512 devices in a mesh: rep: 64 (over x, y, z_hi), fsdp: 8 (over z_lo, core).
Axes of the slice: x: 4, y: 4, z: 16 (z_hi: 4, z_lo: 4; z = z_hi * 4 + z_lo), core: 2. Of those that a mesh axis runs over, the one named last changes fastest.
Arguments:
- activations: bfloat16 [64, 4096, 2048], P('rep', 'fsdp'), may hold values from -6 to 6
- cotangent: bfloat16 [64, 4096, 512], P('rep', 'fsdp'), may hold values from -0.079589844 to 0.079589844
- param: bfloat16 [64, 2048, 512], P('rep', 'fsdp'), may hold values from -0.125 to 0.125
- tracker: bfloat16 [64, 2048, 512], P('rep', 'fsdp'), may hold values from -6 to 6
- prev_grad: bfloat16 [64, 2048, 512], P('rep', 'fsdp'), may hold values from -6 to 6
- moment: bfloat16 [64, 2048, 512], P('rep', 'fsdp'), may hold values from -2 to 2
- second: bfloat16 [64, 2048, 512], P('rep', 'fsdp'), may hold values from 0.099609375 to 2
- step: int32 [1], replicated, may hold values from 0 to 4095
Outputs:
- param_out: bfloat16 [64, 2048, 512], P('rep', 'fsdp')
- tracker_out: bfloat16 [64, 2048, 512], P('rep', 'fsdp')
- moment_out: bfloat16 [64, 2048, 512], P('rep', 'fsdp')
- second_out: bfloat16 [64, 2048, 512], P('rep', 'fsdp')
- grad_out: bfloat16 [64, 2048, 512], P('rep', 'fsdp')
The draws below stay inside these ranges and needn't reach their ends.
Inputs may be any that keep to these rules, and one draw needn't show every extreme that they name: Any step index.
All inputs are finite; a program needn't handle non-finite values.
Results may differ from the reference program's by a relative error of at most 0.014.
Values may be sent and summed in bfloat16 or wider, within the bound.
A program may use at most 64 MiB of HBM per device.

```python
import math
import jax
import jax.numpy as jnp
from jax import lax

D = 2048
C = 512
TOK_DEV = 512
REPS = 64
TOKENS_REP = 4096
N_FSDP = 8


def with_spikes(entries, stream_key, source, target, shards_of, factor):
    owner, partner = [(jnp.arange(entries.shape[position]) // (entries.shape[position] // shards_of)).reshape([-1 if axis == position else 1 for axis in range(entries.ndim)]) for position in (source, target)]
    chosen = jax.random.permutation(stream_key, shards_of)[partner]
    strong = (owner == chosen) | (owner == (partner + shards_of // 2) % shards_of)
    return jnp.where(strong, factor * entries, entries)


def steps_of(stream_key, extent, split, smallest, largest):
    loudness = 1.0
    for axis_at, shards_of in split:
        heights = jax.random.uniform(jax.random.fold_in(jax.random.fold_in(stream_key, 6), axis_at), (shards_of,), jnp.float32, smallest / len(split), largest / len(split))
        loudness = loudness * jnp.repeat(jnp.exp(heights), extent[axis_at] // shards_of).reshape((-1,) + (1,) * (len(extent) - 1 - axis_at))
    return loudness


def scatter_about(stream_key, shape, spread, most, split=(), kind=jnp.bfloat16):
    drawn = spread * jax.random.normal(stream_key, shape, jnp.float32)
    if split:
        drawn = drawn * steps_of(stream_key, shape, split, -0.22, 0.18)
    return jnp.clip(drawn, -most, most).astype(kind)


def heavy_noise(stream_key, extent, spread, reach, cuts, heavy, held_as=jnp.bfloat16):
    values = spread * jax.random.normal(stream_key, extent, jnp.float32)
    if cuts:
        values = values * steps_of(stream_key, extent, cuts, -0.22, 0.18)
    return jnp.clip(with_spikes(values, jax.random.fold_in(stream_key, 3), *heavy), -reach, reach).astype(held_as)


def setup_inputs(seed: int = 0) -> dict:
    seeds = jax.random.split(jax.random.key(seed), 9)
    return {
        "activations": heavy_noise(seeds[0], (REPS, TOKENS_REP, D), 1.0, 6.0, ((0, 64), (1, 8)), (1, 2, 8, 2.0)),
        "cotangent": scatter_about(seeds[1], (REPS, TOKENS_REP, C), 0.0128, 0.079589844, ((0, 64), (1, 8))),
        "param": scatter_about(seeds[2], (REPS, D, C), D ** -0.5, 0.125, ((0, 64), (1, 8))),
        "tracker": scatter_about(seeds[3], (REPS, D, C), 1.0, 6.0, ((0, 64), (1, 8))),
        "prev_grad": scatter_about(seeds[4], (REPS, D, C), 1.0, 6.0, ((0, 64), (1, 8))),
        "moment": scatter_about(seeds[5], (REPS, D, C), 0.3, 2.0, ((0, 64), (1, 8))),
        "second": jnp.clip(jnp.exp(math.log(2.0) - 2.9996462 * jax.random.uniform(seeds[6], (REPS, D, C), jnp.float32) ** steps_of(seeds[6], (REPS, D, C), ((0, 64), (1, 8)), -0.2, 0.2)), 0.099609375, 2.0).astype(jnp.bfloat16),
        "step": jax.random.randint(seeds[7], (1,), 0, 4096).astype(jnp.int32),
    }


beta_one = 0.9
beta_two = 0.95
learn_rate = 0.002
epsilon_value = 1e-08

def replica_grad(pair):
    acts, cotan = pair
    blocks = acts.reshape(N_FSDP, TOK_DEV, D).astype(jnp.float32)
    cotan_blocks = cotan.reshape(N_FSDP, TOK_DEV, C).astype(jnp.float32)
    partial_value = jnp.einsum('ftk,ftc->fkc', blocks, cotan_blocks)
    partial_value = lax.optimization_barrier(partial_value.astype(jnp.bfloat16))
    return lax.optimization_barrier(jnp.sum(partial_value.astype(jnp.float32), axis=0))

def reference(activations, cotangent, param, tracker, prev_grad, moment, second, step):
    grad = lax.map(replica_grad, (activations, cotangent))
    levels = int(math.log2(REPS))
    index = (step[0] % levels).astype(jnp.int32)
    dist = jnp.left_shift(jnp.int32(1), index)
    param_f = param.astype(jnp.float32)
    tracker_f = tracker.astype(jnp.float32)
    mixed_param = 0.5 * (param_f + jnp.roll(param_f, dist, axis=0))
    mixed_tracker = 0.5 * (tracker_f + jnp.roll(tracker_f, dist, axis=0))
    new_tracker = mixed_tracker + grad - prev_grad.astype(jnp.float32)
    new_moment = beta_one * moment.astype(jnp.float32) + (1.0 - beta_one) * new_tracker
    new_second = beta_two * second.astype(jnp.float32) + (1.0 - beta_two) * new_tracker * new_tracker
    count = (step[0] + 1).astype(jnp.float32)
    correct_one = 1.0 - jnp.power(jnp.float32(beta_one), count)
    correct_two = 1.0 - jnp.power(jnp.float32(beta_two), count)
    update = new_moment / correct_one / (jnp.sqrt(new_second / correct_two) + epsilon_value)
    param_out = (mixed_param - learn_rate * update).astype(jnp.bfloat16)
    return (param_out, new_tracker.astype(jnp.bfloat16), new_moment.astype(jnp.bfloat16), new_second.astype(jnp.bfloat16), grad.astype(jnp.bfloat16))
```

```python
import functools

import jax
import jax.numpy as jnp
from jax import lax
from jax.experimental import pallas as pl
from jax.experimental.pallas import tpu as pltpu
from jax.sharding import PartitionSpec as P

beta_one = 0.9
beta_two = 0.95
learn_rate = 0.002
epsilon_value = 1e-08

MESH = pl.DeviceIdType.MESH
CHIPS = 4
PIECES = 4
HALVES = 2
F32 = jnp.float32
BF16 = jnp.bfloat16


def kernel(
    shift,
    scal_ref,
    act_hbm,
    cot_hbm,
    param_hbm,
    tracker_hbm,
    prev_hbm,
    moment_hbm,
    second_hbm,
    param_out,
    tracker_out,
    moment_out,
    second_out,
    grad_out,
    act,
    cot,
    acc,
    mate_send,
    mate_recv,
    line_send,
    line_recv,
    far,
    state,
    result,
    act_sem,
    cot_sem,
    state_sem,
    result_sem,
    mate_ssem,
    mate_rsem,
    line_ssem,
    line_rsem,
    far_ssem,
    far_rsem,
):
    reps = lax.axis_size("rep")
    rep = lax.axis_index("rep")
    col = lax.axis_index("fsdp")
    z = col // 2
    core = col % 2
    mate = (rep, col + 1 - 2 * core)
    far_to = (lax.rem(rep + shift, reps), col)
    far_from = (lax.rem(rep + reps - shift, reps), col)
    rows = param_hbm.shape[0]
    piece = rows // PIECES
    half = rows // HALVES
    last = CHIPS - 1

    upper = z // 2
    inner = (z + upper) % 2
    code = 27 + 72 * inner

    def dest(k):
        plain = (code // (4**k)) % 4 if isinstance(k, int) else lax.shift_right_logical(code, 2 * k) % 4
        return plain + upper * (last - 2 * plain)

    barrier = pltpu.get_barrier_semaphore()
    pl.semaphore_signal(barrier, inc=1, device_id=mate, device_id_type=MESH)

    @pl.when(z > 0)
    def _():
        pl.semaphore_signal(barrier, inc=1, device_id=(rep, col - 2), device_id_type=MESH)

    @pl.when(z < last)
    def _():
        pl.semaphore_signal(barrier, inc=1, device_id=(rep, col + 2), device_id_type=MESH)

    pl.semaphore_signal(barrier, inc=1, device_id=far_from, device_id_type=MESH)
    pl.semaphore_signal(barrier, inc=1, device_id=far_to, device_id_type=MESH)

    def act_load(k):
        start = pl.multiple_of(dest(k) * (2 * rows), 2 * rows)
        return pltpu.make_async_copy(
            act_hbm.at[:, pl.ds(start, 2 * rows)], act.at[k], act_sem.at[k]
        )

    cot_load = pltpu.make_async_copy(cot_hbm, cot, cot_sem)
    cot_load.start()
    act_load(0).start()
    act_load(1).start()
    act_load(2).start()
    act_load(3).start()
    state_loads = [
        pltpu.make_async_copy(ref, state.at[n], state_sem.at[n])
        for n, ref in enumerate((param_hbm, tracker_hbm, prev_hbm, moment_hbm, second_hbm))
    ]
    for load in state_loads:
        load.start()

    far_copies = [
        pltpu.make_async_remote_copy(
            src_ref=ref,
            dst_ref=far.at[n],
            send_sem=far_ssem.at[n],
            recv_sem=far_rsem.at[n],
            device_id=far_to,
            device_id_type=MESH,
        )
        for n, ref in enumerate((param_hbm, tracker_hbm))
    ]

    def mate_copy(k, h):
        part = pl.ds(h * half, half)
        return pltpu.make_async_remote_copy(
            src_ref=mate_send.at[k, part],
            dst_ref=mate_recv.at[k, part],
            send_sem=mate_ssem.at[k, h],
            recv_sem=mate_rsem.at[k, h],
            device_id=mate,
            device_id_type=MESH,
        )

    def term(k, which):
        columns = pl.ds(pl.multiple_of(which * rows, rows), rows)
        return lax.dot_general(
            act[k, :, columns], cot[...], (((0,), (0,)), ((), ())), preferred_element_type=F32
        )

    def line_copy(k, p):
        d = dest(k)
        way = jnp.where(d > z, 1, -1)
        slot = jnp.where((d == z + way) & (way < 0), CHIPS, d)
        part = pl.ds(p * piece, piece)
        return pltpu.make_async_remote_copy(
            src_ref=line_send.at[k, part],
            dst_ref=line_recv.at[slot, part],
            send_sem=line_ssem.at[k, p],
            recv_sem=line_rsem.at[slot, p],
            device_id=(rep, col + 2 * way),
            device_id_type=MESH,
        )

    def arrival(slot, p):
        part = pl.ds(p * piece, piece)
        return pltpu.make_async_remote_copy(
            src_ref=line_send.at[0, part],
            dst_ref=line_recv.at[slot, part],
            send_sem=line_ssem.at[0, p],
            recv_sem=line_rsem.at[slot, p],
            device_id=mate,
            device_id_type=MESH,
        )

    def wait_barrier():
        ends = jnp.where(z > 0, 1, 0) + jnp.where(z < last, 1, 0)
        pl.semaphore_wait(barrier, 3 + ends)

    def compute(k):
        act_load(k).wait()
        mate_send[k] = term(k, 1 - core).astype(BF16)

        @pl.when(k == 0)
        def _():
            wait_barrier()

        for h in range(HALVES):
            mate_copy(k, h).start()

        @pl.when(k == 0)
        def _():
            for copy in far_copies:
                copy.start()

        acc[k] = term(k, core)

    def pass_on(k):
        d = dest(k)
        way = jnp.where(d > z, 1, -1)
        behind = z - way
        fed = (behind >= 0) & (behind <= last)
        for p in range(PIECES):
            part = pl.ds(p * piece, piece)
            if p % (PIECES // HALVES) == 0:
                mate_copy(k, p // (PIECES // HALVES)).wait_recv()
            own = acc[k, part] + mate_recv[k, part].astype(F32)

            @pl.when(fed)
            def _():
                arrival(d, p).wait_recv()
                line_send[k, part] = (own + line_recv[d, part].astype(F32)).astype(BF16)

            @pl.when(jnp.logical_not(fed))
            def _():
                line_send[k, part] = own.astype(BF16)

            line_copy(k, p).start()

    cot_load.wait()

    def step(i, carry):
        @pl.when(i < CHIPS)
        def _():
            compute(i)

        @pl.when((i >= 1) & (i < CHIPS))
        def _():
            pass_on(i - 1)

        return carry

    lax.fori_loop(0, CHIPS, step, 0)

    for load in state_loads:
        load.wait()
    for copy in far_copies:
        copy.wait_recv()
    scale_one = scal_ref[0]
    scale_two = scal_ref[1]

    def result_copy(n, ref, p):
        part = pl.ds(p * piece, piece)
        return pltpu.make_async_copy(result.at[n, part], ref.at[part], result_sem.at[n, p])

    outs = (param_out, tracker_out, moment_out, second_out, grad_out)

    def finish(p, carry):
        part = pl.ds(pl.multiple_of(p * piece, piece), piece)

        @pl.when(p % (PIECES // HALVES) == 0)
        def _():
            mate_copy(last, p // (PIECES // HALVES)).wait_recv()

        acc[last, part] += mate_recv[last, part].astype(F32)

        @pl.when(z > 0)
        def _():
            arrival(z, p).wait_recv()
            acc[last, part] += line_recv[z, part].astype(F32)

        @pl.when(z < last)
        def _():
            arrival(CHIPS, p).wait_recv()
            acc[last, part] += line_recv[CHIPS, part].astype(F32)

        grad = acc[last, part]
        mixed_param = 0.5 * (state[0, part].astype(F32) + far[0, part].astype(F32))
        mixed_tracker = 0.5 * (state[1, part].astype(F32) + far[1, part].astype(F32))
        new_tracker = mixed_tracker + grad - state[2, part].astype(F32)
        new_moment = beta_one * state[3, part].astype(F32) + (1.0 - beta_one) * new_tracker
        new_second = (
            beta_two * state[4, part].astype(F32) + (1.0 - beta_two) * new_tracker * new_tracker
        )
        update = (new_moment * scale_one) / (jnp.sqrt(new_second * scale_two) + epsilon_value)
        values = (mixed_param - learn_rate * update, new_tracker, new_moment, new_second, grad)
        for n, value in enumerate(values):
            result[n, part] = value.astype(BF16)
        for n, ref in enumerate(outs):
            result_copy(n, ref, p).start()
        return carry

    lax.fori_loop(0, PIECES, finish, 0)

    for n, ref in enumerate(outs):
        for p in range(PIECES):
            result_copy(n, ref, p).wait()
    for copy in far_copies:
        copy.wait_send()
    for k in range(CHIPS):
        for h in range(HALVES):
            mate_copy(k, h).wait_send()
    for k in range(CHIPS - 1):
        for p in range(PIECES):
            line_copy(k, p).wait_send()


def step_at(index, scal, act, cot, param, tracker, prev, moment, second):
    tokens, width = act.shape
    rows, columns = param.shape
    out = jax.ShapeDtypeStruct((rows, columns), BF16)
    anywhere = pl.BlockSpec(memory_space=pl.ANY)
    dma = pltpu.SemaphoreType.DMA
    return pl.pallas_call(
        functools.partial(kernel, 1 << index),
        out_shape=[out] * 5,
        in_specs=[pl.BlockSpec(memory_space=pltpu.SMEM)] + [anywhere] * 7,
        out_specs=[anywhere] * 5,
        scratch_shapes=[
            pltpu.VMEM((CHIPS, tokens, 2 * rows), BF16),
            pltpu.VMEM((tokens, columns), BF16),
            pltpu.VMEM((CHIPS, rows, columns), F32),
            pltpu.VMEM((CHIPS, rows, columns), BF16),
            pltpu.VMEM((CHIPS, rows, columns), BF16),
            pltpu.VMEM((CHIPS - 1, rows, columns), BF16),
            pltpu.VMEM((CHIPS + 1, rows, columns), BF16),
            pltpu.VMEM((2, rows, columns), BF16),
            pltpu.VMEM((5, rows, columns), BF16),
            pltpu.VMEM((5, rows, columns), BF16),
            dma((CHIPS,)),
            dma,
            dma((5,)),
            dma((5, PIECES)),
            dma((CHIPS, HALVES)),
            dma((CHIPS, HALVES)),
            dma((CHIPS - 1, PIECES)),
            dma((CHIPS + 1, PIECES)),
            dma((2,)),
            dma((2,)),
        ],
        compiler_params=pltpu.CompilerParams(
            collective_id=index, has_side_effects=True, vmem_limit_bytes=40 * 2**20
        ),
        name=f"step_{index}",
    )(scal, act, cot, param, tracker, prev, moment, second)


def settle_kernel(*refs):
    ins, outs, bufs, isem, osem = refs[:5], refs[5:10], refs[10], refs[11], refs[12]
    loads = [pltpu.make_async_copy(ref, bufs.at[n], isem.at[n]) for n, ref in enumerate(ins)]
    stores = [pltpu.make_async_copy(bufs.at[n], ref, osem.at[n]) for n, ref in enumerate(outs)]
    for load in loads:
        load.start()
    for load, store in zip(loads, stores):
        load.wait()
        store.start()
    for store in stores:
        store.wait()


def settle(values):
    rows, columns = values[0].shape
    anywhere = pl.BlockSpec(memory_space=pl.ANY)
    return pl.pallas_call(
        settle_kernel,
        out_shape=[jax.ShapeDtypeStruct((rows, columns), BF16)] * 5,
        in_specs=[anywhere] * 5,
        out_specs=[anywhere] * 5,
        scratch_shapes=[
            pltpu.VMEM((5, rows, columns), BF16),
            pltpu.SemaphoreType.DMA((5,)),
            pltpu.SemaphoreType.DMA((5,)),
        ],
        compiler_params=pltpu.CompilerParams(vmem_limit_bytes=4 * 2**20),
        name="settle",
    )(*values)


def body(activations, cotangent, param, tracker, prev_grad, moment, second, step):
    levels = lax.axis_size("rep").bit_length() - 1
    count = (step[0] + 1).astype(F32)
    correct_one = 1.0 - jnp.power(jnp.float32(beta_one), count)
    correct_two = 1.0 - jnp.power(jnp.float32(beta_two), count)
    scal = jnp.stack([1.0 / correct_one, 1.0 / correct_two])
    values = lax.switch(
        step[0] % levels,
        [functools.partial(step_at, index) for index in range(levels)],
        scal,
        activations[0],
        cotangent[0],
        param[0],
        tracker[0],
        prev_grad[0],
        moment[0],
        second[0],
    )
    return tuple(value[None] for value in settle(values))


def solution(mesh):
    spread = P("rep", "fsdp", None)
    return jax.shard_map(
        body,
        mesh=mesh,
        in_specs=(spread,) * 7 + (P(),),
        out_specs=(spread,) * 5,
        check_vma=False,
    )
```

```python
import functools
import math

import jax
import jax.numpy as jnp
from jax import lax
from jax.experimental import pallas as pl
from jax.experimental.pallas import tpu as pltpu
from jax.sharding import PartitionSpec as P

beta_one = 0.9
beta_two = 0.95
learn_rate = 0.002
epsilon_value = 1e-08

MESH = pl.DeviceIdType.MESH
CHIPS = 4
PIECES = 4
HALVES = 2
ALONG_Z = 2
GROUPS = 4
F32 = jnp.float32
BF16 = jnp.bfloat16


def kernel(
    index,
    step_hbm,
    act_hbm,
    cot_hbm,
    param_hbm,
    tracker_hbm,
    prev_hbm,
    moment_hbm,
    second_hbm,
    param_out,
    tracker_out,
    moment_out,
    second_out,
    grad_out,
    act,
    cot,
    acc,
    mate_send,
    mate_recv,
    line_send,
    line_recv,
    far,
    state,
    relay,
    step_smem,
    act_sem,
    cot_sem,
    state_sem,
    step_sem,
    mate_ssem,
    mate_rsem,
    line_ssem,
    line_rsem,
    far_ssem,
    far_rsem,
    relay_ssem,
    relay_rsem,
    ready,
):
    reps = lax.axis_size("rep")
    rep = lax.axis_index("rep")
    col = lax.axis_index("fsdp")
    z = col // 2
    core = col % 2
    mate = (rep, col + 1 - 2 * core)
    shift = 1 << index
    far_to = (lax.rem(rep + shift, reps), col)
    far_from = (lax.rem(rep + reps - shift, reps), col)
    rows = param_hbm.shape[0]
    piece = rows // PIECES
    half = rows // HALVES
    last = CHIPS - 1

    upper = z // 2
    inner = (z + upper) % 2
    code = 27 + 72 * inner

    def dest(k):
        plain = (code // (4**k)) % 4 if isinstance(k, int) else lax.shift_right_logical(code, 2 * k) % 4
        return plain + upper * (last - 2 * plain)

    barrier = pltpu.get_barrier_semaphore()
    pl.semaphore_signal(barrier, inc=1, device_id=mate, device_id_type=MESH)

    @pl.when(z > 0)
    def _():
        pl.semaphore_signal(barrier, inc=1, device_id=(rep, col - 2), device_id_type=MESH)

    @pl.when(z < last)
    def _():
        pl.semaphore_signal(barrier, inc=1, device_id=(rep, col + 2), device_id_type=MESH)

    relayed = index == 0
    if relayed:
        level = rep % GROUPS
        top = GROUPS - 1
        ring = rep - level
        below = (ring + (level + GROUPS - 1) % GROUPS, col)
        above = (ring + (level + 1) % GROUPS, col)
        finally_to = ((ring + (level + GROUPS - 2) % GROUPS + shift) % reps, col)
        origin = (rep + reps - shift) % reps
        brought_by = (origin - origin % GROUPS + (origin + 2) % GROUPS, col)
        expected = 1 + jnp.where(level > 0, 3, 0) + jnp.where(level == top, 3, 0)

        @pl.when(level < top)
        def _():
            for device in (far_to, above, brought_by):
                pl.semaphore_signal(barrier, inc=1, device_id=device, device_id_type=MESH)

        @pl.when(level == 0)
        def _():
            for device in (far_from, below, finally_to):
                pl.semaphore_signal(barrier, inc=1, device_id=device, device_id_type=MESH)

    else:
        expected = 2
        pl.semaphore_signal(barrier, inc=1, device_id=far_from, device_id_type=MESH)

    def act_load(k, own):
        side = 1 - core if own == 0 else core
        start = pl.multiple_of((2 * dest(k) + side) * rows, rows)
        return pltpu.make_async_copy(
            act_hbm.at[:, pl.ds(start, rows)], act.at[k, own], act_sem.at[k, own]
        )

    cot_load = pltpu.make_async_copy(cot_hbm, cot, cot_sem)
    cot_load.start()
    act_load(0, 0).start()
    act_load(0, 1).start()
    state_loads = [
        pltpu.make_async_copy(ref, state.at[n], state_sem.at[n])
        for n, ref in enumerate((param_hbm, tracker_hbm, prev_hbm, moment_hbm, second_hbm))
    ]
    step_load = pltpu.make_async_copy(step_hbm, step_smem, step_sem)

    def later_loads():
        for k in range(1, CHIPS):
            for own in range(2):
                act_load(k, own).start()
            if k == 1:
                for load in state_loads[:2]:
                    load.start()
        for load in state_loads[2:]:
            load.start()
        step_load.start()

    def far_copy(n, p):
        part = pl.ds(p * piece, piece)
        return pltpu.make_async_remote_copy(
            src_ref=state.at[n, part],
            dst_ref=far.at[n, part],
            send_sem=far_ssem.at[n, p],
            recv_sem=far_rsem.at[n, p],
            device_id=far_to,
            device_id_type=MESH,
        )

    def mate_copy(k, h):
        part = pl.ds(h * half, half)
        return pltpu.make_async_remote_copy(
            src_ref=mate_send.at[k, part],
            dst_ref=mate_recv.at[k, part],
            send_sem=mate_ssem.at[k, h],
            recv_sem=mate_rsem.at[k, h],
            device_id=mate,
            device_id_type=MESH,
        )

    def relay_copy(hop, n):
        part = pl.ds((PIECES - 1) * piece, piece)
        ends = hop == GROUPS - 2
        return pltpu.make_async_remote_copy(
            src_ref=relay.at[hop - 1, n] if hop else state.at[n, part],
            dst_ref=far.at[n, part] if ends else relay.at[hop, n],
            send_sem=relay_ssem.at[hop, n],
            recv_sem=far_rsem.at[n, PIECES - 1] if ends else relay_rsem.at[hop, n],
            device_id=finally_to if ends else below,
            device_id_type=MESH,
        )

    def term(k, own):
        return lax.dot_general(
            act[k, own], cot[...], (((0,), (0,)), ((), ())), preferred_element_type=F32
        )

    def line_copy(k, p):
        d = dest(k)
        way = jnp.where(d > z, 1, -1)
        slot = jnp.where((d == z + way) & (way < 0), CHIPS, d)
        part = pl.ds(p * piece, piece)
        return pltpu.make_async_remote_copy(
            src_ref=line_send.at[k, part],
            dst_ref=line_recv.at[slot, part],
            send_sem=line_ssem.at[k, p],
            recv_sem=line_rsem.at[slot, p],
            device_id=(rep, col + 2 * way),
            device_id_type=MESH,
        )

    def arrival(slot, p):
        part = pl.ds(p * piece, piece)
        return pltpu.make_async_remote_copy(
            src_ref=line_send.at[0, part],
            dst_ref=line_recv.at[slot, part],
            send_sem=line_ssem.at[0, p],
            recv_sem=line_rsem.at[slot, p],
            device_id=mate,
            device_id_type=MESH,
        )

    def wait_barrier():
        ends = jnp.where(z > 0, 1, 0) + jnp.where(z < last, 1, 0)
        pl.semaphore_wait(barrier, expected + ends)
        if relayed:

            @pl.when(level > 0)
            def _():
                pl.semaphore_signal(ready, inc=1, device_id=far_from, device_id_type=MESH)

            @pl.when(level == top)
            def _():
                for device in (above, brought_by):
                    pl.semaphore_signal(ready, inc=1, device_id=device, device_id_type=MESH)

    def compute(k):
        act_load(k, 0).wait()

        @pl.when(k == 0)
        def _():
            later_loads()

        mate_send[k] = term(k, 0).astype(BF16)

        @pl.when(k == 0)
        def _():
            wait_barrier()

        for h in range(HALVES):
            mate_copy(k, h).start()

        act_load(k, 1).wait()
        acc[k] = term(k, 1)

        @pl.when(k == 1)
        def _():
            for load in state_loads[:2]:
                load.wait()
            if relayed:

                @pl.when(level > 0)
                def _():
                    for n in range(2):
                        relay_copy(0, n).start()

            if index >= ALONG_Z:
                for n in range(2):
                    for p in range(PIECES):
                        far_copy(n, p).start()

    def pass_on(k):
        d = dest(k)
        way = jnp.where(d > z, 1, -1)
        behind = z - way
        fed = (behind >= 0) & (behind <= last)
        for p in range(PIECES):
            part = pl.ds(p * piece, piece)
            if p % (PIECES // HALVES) == 0:
                mate_copy(k, p // (PIECES // HALVES)).wait_recv()
            own = acc[k, part] + mate_recv[k, part].astype(F32)

            @pl.when(fed)
            def _():
                arrival(d, p).wait_recv()
                line_send[k, part] = (own + line_recv[d, part].astype(F32)).astype(BF16)

            @pl.when(jnp.logical_not(fed))
            def _():
                line_send[k, part] = own.astype(BF16)

            line_copy(k, p).start()
            if index < ALONG_Z and not relayed:
                turn = k * PIECES + p

                @pl.when(turn < 2 * PIECES)
                def _():
                    far_copy(turn % 2, turn // 2).start()

        if relayed:

            @pl.when((k == 0) & (level > 0) & (level < top))
            def _():
                pl.semaphore_wait(ready, 1)

            @pl.when(level > 0)
            def _():
                for n in range(2):
                    far_copy(n, k).start()

            @pl.when((k == 1) & (level > 0))
            def _():
                for n in range(2):
                    relay_copy(0, n).wait_recv()
                    relay_copy(1, n).start()

            @pl.when((k == 2) & (level == 0))
            def _():
                pl.semaphore_wait(ready, 3)
                for n in range(2):
                    relay_copy(0, n).start()
                for p in range(PIECES - 1):
                    for n in range(2):
                        far_copy(n, p).start()
                for n in range(2):
                    relay_copy(0, n).wait_recv()
                    relay_copy(1, n).start()

            @pl.when(k == 2)
            def _():
                for n in range(2):
                    relay_copy(1, n).wait_recv()
                    relay_copy(2, n).start()

    cot_load.wait()

    def step(i, carry):
        @pl.when(i < CHIPS)
        def _():
            compute(i)

        @pl.when((i >= 1) & (i < CHIPS))
        def _():
            pass_on(i - 1)

        return carry

    lax.fori_loop(0, CHIPS, step, 0)

    for load in state_loads[2:]:
        load.wait()
    step_load.wait()
    count = jnp.full((1, param_hbm.shape[1]), step_smem[0] + 1, jnp.int32).astype(F32)
    scale_one = 1.0 / (1.0 - jnp.exp(count * math.log(beta_one)))
    scale_two = 1.0 / (1.0 - jnp.exp(count * math.log(beta_two)))

    def finish(p, carry):
        part = pl.ds(pl.multiple_of(p * piece, piece), piece)

        for n in range(2):
            far_copy(n, p).wait_recv()

        @pl.when(p % (PIECES // HALVES) == 0)
        def _():
            mate_copy(last, p // (PIECES // HALVES)).wait_recv()

        acc[last, part] += mate_recv[last, part].astype(F32)

        @pl.when(z > 0)
        def _():
            arrival(z, p).wait_recv()
            acc[last, part] += line_recv[z, part].astype(F32)

        @pl.when(z < last)
        def _():
            arrival(CHIPS, p).wait_recv()
            acc[last, part] += line_recv[CHIPS, part].astype(F32)

        grad = acc[last, part]
        mixed_param = 0.5 * (state[0, part].astype(F32) + far[0, part].astype(F32))
        mixed_tracker = 0.5 * (state[1, part].astype(F32) + far[1, part].astype(F32))
        new_tracker = mixed_tracker + grad - state[2, part].astype(F32)
        new_moment = beta_one * state[3, part].astype(F32) + (1.0 - beta_one) * new_tracker
        new_second = (
            beta_two * state[4, part].astype(F32) + (1.0 - beta_two) * new_tracker * new_tracker
        )
        update = (new_moment * scale_one) / (jnp.sqrt(new_second * scale_two) + epsilon_value)
        param_out[part] = (mixed_param - learn_rate * update).astype(BF16)
        tracker_out[part] = new_tracker.astype(BF16)
        moment_out[part] = new_moment.astype(BF16)
        second_out[part] = new_second.astype(BF16)
        grad_out[part] = grad.astype(BF16)
        return carry

    lax.fori_loop(0, PIECES, finish, 0)

    for n in range(2):
        for p in range(PIECES):
            if relayed and p == PIECES - 1:
                for hop in range(GROUPS - 1):
                    relay_copy(hop, n).wait_send()
            else:
                far_copy(n, p).wait_send()
    for k in range(CHIPS):
        for h in range(HALVES):
            mate_copy(k, h).wait_send()
    for k in range(CHIPS - 1):
        for p in range(PIECES):
            line_copy(k, p).wait_send()


def step_at(index, step, act, cot, param, tracker, prev, moment, second):
    tokens, width = act.shape
    rows, columns = param.shape
    out = jax.ShapeDtypeStruct((rows, columns), BF16)
    anywhere = pl.BlockSpec(memory_space=pl.ANY)
    dma = pltpu.SemaphoreType.DMA
    return pl.pallas_call(
        functools.partial(kernel, index),
        out_shape=[out] * 5,
        in_specs=[anywhere] * 8,
        out_specs=[pl.BlockSpec(memory_space=pltpu.VMEM)] * 5,
        scratch_shapes=[
            pltpu.VMEM((CHIPS, 2, tokens, rows), BF16),
            pltpu.VMEM((tokens, columns), BF16),
            pltpu.VMEM((CHIPS, rows, columns), F32),
            pltpu.VMEM((CHIPS, rows, columns), BF16),
            pltpu.VMEM((CHIPS, rows, columns), BF16),
            pltpu.VMEM((CHIPS - 1, rows, columns), BF16),
            pltpu.VMEM((CHIPS + 1, rows, columns), BF16),
            pltpu.VMEM((2, rows, columns), BF16),
            pltpu.VMEM((5, rows, columns), BF16),
            pltpu.VMEM((2, 2, rows // PIECES, columns), BF16),
            pltpu.SMEM((1,), jnp.int32),
            dma((CHIPS, 2)),
            dma,
            dma((5,)),
            dma,
            dma((CHIPS, HALVES)),
            dma((CHIPS, HALVES)),
            dma((CHIPS - 1, PIECES)),
            dma((CHIPS + 1, PIECES)),
            dma((2, PIECES)),
            dma((2, PIECES)),
            dma((GROUPS - 1, 2)),
            dma((GROUPS - 2, 2)),
            pltpu.SemaphoreType.REGULAR,
        ],
        compiler_params=pltpu.CompilerParams(
            collective_id=index, has_side_effects=True, vmem_limit_bytes=40 * 2**20
        ),
        name=f"step_{index}",
    )(step, act, cot, param, tracker, prev, moment, second)


def settle_kernel(*refs):
    ins, outs, sem = refs[:5], refs[5:10], refs[10]
    copies = [
        pltpu.make_async_copy(ins[n], outs[n], sem.at[n]) for n in range(5)
    ]
    for copy in copies:
        copy.start()
    for copy in copies:
        copy.wait()


def settle(values):
    rows, columns = values[0].shape
    return pl.pallas_call(
        settle_kernel,
        out_shape=[jax.ShapeDtypeStruct((rows, columns), BF16)] * 5,
        in_specs=[pl.BlockSpec(memory_space=pltpu.VMEM)] * 5,
        out_specs=[pl.BlockSpec(memory_space=pl.ANY)] * 5,
        scratch_shapes=[pltpu.SemaphoreType.DMA((5,))],
        compiler_params=pltpu.CompilerParams(vmem_limit_bytes=4 * 2**20),
        name="settle",
    )(*values)


def body(activations, cotangent, param, tracker, prev_grad, moment, second, step):
    levels = lax.axis_size("rep").bit_length() - 1
    values = lax.switch(
        step[0] % levels,
        [functools.partial(step_at, index) for index in range(levels)],
        step,
        activations[0],
        cotangent[0],
        param[0],
        tracker[0],
        prev_grad[0],
        moment[0],
        second[0],
    )
    return tuple(value[None] for value in settle(values))


def solution(mesh):
    spread = P("rep", "fsdp", None)
    return jax.shard_map(
        body,
        mesh=mesh,
        in_specs=(spread,) * 7 + (P(),),
        out_specs=(spread,) * 5,
        check_vma=False,
    )
```

```python
import functools
import math

import jax
import jax.numpy as jnp
from jax import lax
from jax.experimental import pallas as pl
from jax.experimental.pallas import tpu as pltpu
from jax.sharding import PartitionSpec as P

beta_one = 0.9
beta_two = 0.95
learn_rate = 0.002
epsilon_value = 1e-08

MESH = pl.DeviceIdType.MESH
CHIPS = 4
PIECES = 4
HALVES = 2
ALONG_Z = 2
GROUPS = 4
F32 = jnp.float32
BF16 = jnp.bfloat16


def kernel(
    index,
    step_hbm,
    act_hbm,
    cot_hbm,
    param_hbm,
    tracker_hbm,
    prev_hbm,
    moment_hbm,
    second_hbm,
    param_out,
    tracker_out,
    moment_out,
    second_out,
    grad_out,
    act,
    cot,
    acc,
    mate_send,
    mate_recv,
    line_send,
    line_recv,
    far,
    state,
    relay,
    step_smem,
    act_sem,
    cot_sem,
    state_sem,
    step_sem,
    mate_ssem,
    mate_rsem,
    line_ssem,
    line_rsem,
    far_ssem,
    far_rsem,
    relay_ssem,
    relay_rsem,
    ready,
):
    reps = lax.axis_size("rep")
    rep = lax.axis_index("rep")
    col = lax.axis_index("fsdp")
    z = col // 2
    core = col % 2
    mate = (rep, col + 1 - 2 * core)
    shift = 1 << index
    far_to = (lax.rem(rep + shift, reps), col)
    far_from = (lax.rem(rep + reps - shift, reps), col)
    rows = param_hbm.shape[0]
    piece = rows // PIECES
    half = rows // HALVES
    last = CHIPS - 1

    upper = z // 2
    inner = (z + upper) % 2
    code = 27 + 72 * inner

    def dest(k):
        plain = (code // (4**k)) % 4 if isinstance(k, int) else lax.shift_right_logical(code, 2 * k) % 4
        return plain + upper * (last - 2 * plain)

    barrier = pltpu.get_barrier_semaphore()
    pl.semaphore_signal(barrier, inc=1, device_id=mate, device_id_type=MESH)

    @pl.when(z > 0)
    def _():
        pl.semaphore_signal(barrier, inc=1, device_id=(rep, col - 2), device_id_type=MESH)

    @pl.when(z < last)
    def _():
        pl.semaphore_signal(barrier, inc=1, device_id=(rep, col + 2), device_id_type=MESH)

    relayed = index == 0
    if relayed:
        level = rep % GROUPS
        top = GROUPS - 1
        ring = rep - level
        below = (ring + (level + GROUPS - 1) % GROUPS, col)
        above = (ring + (level + 1) % GROUPS, col)
        finally_to = ((ring + (level + GROUPS - 2) % GROUPS + shift) % reps, col)
        origin = (rep + reps - shift) % reps
        brought_by = (origin - origin % GROUPS + (origin + 2) % GROUPS, col)
        expected = 1 + jnp.where(level > 0, 3, 0) + jnp.where(level == top, 3, 0)

        @pl.when(level < top)
        def _():
            for device in (far_to, above, brought_by):
                pl.semaphore_signal(barrier, inc=1, device_id=device, device_id_type=MESH)

        @pl.when(level == 0)
        def _():
            for device in (far_from, below, finally_to):
                pl.semaphore_signal(barrier, inc=1, device_id=device, device_id_type=MESH)

    else:
        expected = 2
        pl.semaphore_signal(barrier, inc=1, device_id=far_from, device_id_type=MESH)

    def act_load(k, own):
        side = 1 - core if own == 0 else core
        start = pl.multiple_of((2 * dest(k) + side) * rows, rows)
        return pltpu.make_async_copy(
            act_hbm.at[:, pl.ds(start, rows)], act.at[k, own], act_sem.at[k, own]
        )

    cot_load = pltpu.make_async_copy(cot_hbm, cot, cot_sem)
    cot_load.start()
    act_load(0, 0).start()
    act_load(0, 1).start()
    state_loads = [
        pltpu.make_async_copy(ref, state.at[n], state_sem.at[n])
        for n, ref in enumerate((param_hbm, tracker_hbm, prev_hbm, moment_hbm, second_hbm))
    ]
    step_load = pltpu.make_async_copy(step_hbm, step_smem, step_sem)

    def later_loads():
        for k in range(1, CHIPS):
            for own in range(2):
                act_load(k, own).start()
            if k == 1:
                for load in state_loads[:2]:
                    load.start()
        for load in state_loads[2:]:
            load.start()
        step_load.start()

    def far_copy(n, p):
        part = pl.ds(p * piece, piece)
        return pltpu.make_async_remote_copy(
            src_ref=state.at[n, part],
            dst_ref=far.at[n, part],
            send_sem=far_ssem.at[n, p],
            recv_sem=far_rsem.at[n, p],
            device_id=far_to,
            device_id_type=MESH,
        )

    def mate_copy(k, h):
        part = pl.ds(h * half, half)
        return pltpu.make_async_remote_copy(
            src_ref=mate_send.at[k, part],
            dst_ref=mate_recv.at[k, part],
            send_sem=mate_ssem.at[k, h],
            recv_sem=mate_rsem.at[k, h],
            device_id=mate,
            device_id_type=MESH,
        )

    def relay_copy(hop, n):
        part = pl.ds((PIECES - 1) * piece, piece)
        ends = hop == GROUPS - 2
        return pltpu.make_async_remote_copy(
            src_ref=relay.at[hop - 1, n] if hop else state.at[n, part],
            dst_ref=far.at[n, part] if ends else relay.at[hop, n],
            send_sem=relay_ssem.at[hop, n],
            recv_sem=far_rsem.at[n, PIECES - 1] if ends else relay_rsem.at[hop, n],
            device_id=finally_to if ends else below,
            device_id_type=MESH,
        )

    def term(k, own):
        return lax.dot_general(
            act[k, own], cot[...], (((0,), (0,)), ((), ())), preferred_element_type=F32
        )

    def line_copy(k, p):
        d = dest(k)
        way = jnp.where(d > z, 1, -1)
        slot = jnp.where((d == z + way) & (way < 0), CHIPS, d)
        part = pl.ds(p * piece, piece)
        return pltpu.make_async_remote_copy(
            src_ref=line_send.at[k, part],
            dst_ref=line_recv.at[slot, part],
            send_sem=line_ssem.at[k, p],
            recv_sem=line_rsem.at[slot, p],
            device_id=(rep, col + 2 * way),
            device_id_type=MESH,
        )

    def arrival(slot, p):
        part = pl.ds(p * piece, piece)
        return pltpu.make_async_remote_copy(
            src_ref=line_send.at[0, part],
            dst_ref=line_recv.at[slot, part],
            send_sem=line_ssem.at[0, p],
            recv_sem=line_rsem.at[slot, p],
            device_id=mate,
            device_id_type=MESH,
        )

    def wait_barrier():
        ends = jnp.where(z > 0, 1, 0) + jnp.where(z < last, 1, 0)
        pl.semaphore_wait(barrier, expected + ends)
        if relayed:

            @pl.when(level > 0)
            def _():
                pl.semaphore_signal(ready, inc=1, device_id=far_from, device_id_type=MESH)

            @pl.when(level == top)
            def _():
                for device in (above, brought_by):
                    pl.semaphore_signal(ready, inc=1, device_id=device, device_id_type=MESH)

    def compute(k):
        act_load(k, 0).wait()

        @pl.when(k == 0)
        def _():
            later_loads()

        mate_send[k] = term(k, 0).astype(BF16)

        @pl.when(k == 0)
        def _():
            wait_barrier()

        for h in range(HALVES):
            mate_copy(k, h).start()

        act_load(k, 1).wait()
        acc[k] = term(k, 1)

        @pl.when(k == 1)
        def _():
            for load in state_loads[:2]:
                load.wait()
            if relayed:

                @pl.when(level > 0)
                def _():
                    for n in range(2):
                        relay_copy(0, n).start()

            if index >= ALONG_Z:
                for n in range(2):
                    for p in range(PIECES):
                        far_copy(n, p).start()

    def pass_on(k):
        d = dest(k)
        way = jnp.where(d > z, 1, -1)
        behind = z - way
        fed = (behind >= 0) & (behind <= last)
        for p in range(PIECES):
            part = pl.ds(p * piece, piece)
            if p % (PIECES // HALVES) == 0:
                mate_copy(k, p // (PIECES // HALVES)).wait_recv()
            own = acc[k, part] + mate_recv[k, part].astype(F32)

            @pl.when(fed)
            def _():
                arrival(d, p).wait_recv()
                line_send[k, part] = (own + line_recv[d, part].astype(F32)).astype(BF16)

            @pl.when(jnp.logical_not(fed))
            def _():
                line_send[k, part] = own.astype(BF16)

            line_copy(k, p).start()
            if index < ALONG_Z and not relayed:
                turn = k * PIECES + p

                @pl.when(turn < 2 * PIECES)
                def _():
                    far_copy(turn % 2, turn // 2).start()

        if relayed:

            @pl.when((k == 0) & (level > 0) & (level < top))
            def _():
                pl.semaphore_wait(ready, 1)

            @pl.when((level > 0) & (k == 0))
            def _():
                for p in range(PIECES - 1):
                    for n in range(2):
                        far_copy(n, p).start()

            @pl.when((k == 1) & (level > 0))
            def _():
                for n in range(2):
                    relay_copy(0, n).wait_recv()
                    relay_copy(1, n).start()

            @pl.when((k == 1) & (level == 0))
            def _():
                pl.semaphore_wait(ready, 3)
                for n in range(2):
                    relay_copy(0, n).start()
                for p in range(PIECES - 1):
                    for n in range(2):
                        far_copy(n, p).start()

            @pl.when((k == 2) & (level == 0))
            def _():
                for n in range(2):
                    relay_copy(0, n).wait_recv()
                    relay_copy(1, n).start()

            @pl.when(k == 2)
            def _():
                for n in range(2):
                    relay_copy(1, n).wait_recv()
                    relay_copy(2, n).start()

    cot_load.wait()

    def step(i, carry):
        @pl.when(i < CHIPS)
        def _():
            compute(i)

        @pl.when((i >= 1) & (i < CHIPS))
        def _():
            pass_on(i - 1)

        return carry

    lax.fori_loop(0, CHIPS, step, 0)

    for load in state_loads[2:]:
        load.wait()
    step_load.wait()
    count = jnp.full((1, param_hbm.shape[1]), step_smem[0] + 1, jnp.int32).astype(F32)
    scale_one = 1.0 / (1.0 - jnp.exp(count * math.log(beta_one)))
    scale_two = 1.0 / (1.0 - jnp.exp(count * math.log(beta_two)))

    def finish(p, carry):
        part = pl.ds(pl.multiple_of(p * piece, piece), piece)

        for n in range(2):
            far_copy(n, p).wait_recv()

        @pl.when(p % (PIECES // HALVES) == 0)
        def _():
            mate_copy(last, p // (PIECES // HALVES)).wait_recv()

        acc[last, part] += mate_recv[last, part].astype(F32)

        @pl.when(z > 0)
        def _():
            arrival(z, p).wait_recv()
            acc[last, part] += line_recv[z, part].astype(F32)

        @pl.when(z < last)
        def _():
            arrival(CHIPS, p).wait_recv()
            acc[last, part] += line_recv[CHIPS, part].astype(F32)

        grad = acc[last, part]
        mixed_param = 0.5 * (state[0, part].astype(F32) + far[0, part].astype(F32))
        mixed_tracker = 0.5 * (state[1, part].astype(F32) + far[1, part].astype(F32))
        new_tracker = mixed_tracker + grad - state[2, part].astype(F32)
        new_moment = beta_one * state[3, part].astype(F32) + (1.0 - beta_one) * new_tracker
        new_second = (
            beta_two * state[4, part].astype(F32) + (1.0 - beta_two) * new_tracker * new_tracker
        )
        update = (new_moment * scale_one) / (jnp.sqrt(new_second * scale_two) + epsilon_value)
        param_out[part] = (mixed_param - learn_rate * update).astype(BF16)
        tracker_out[part] = new_tracker.astype(BF16)
        moment_out[part] = new_moment.astype(BF16)
        second_out[part] = new_second.astype(BF16)
        grad_out[part] = grad.astype(BF16)
        return carry

    lax.fori_loop(0, PIECES, finish, 0)

    for n in range(2):
        for p in range(PIECES):
            if relayed and p == PIECES - 1:
                for hop in range(GROUPS - 1):
                    relay_copy(hop, n).wait_send()
            else:
                far_copy(n, p).wait_send()
    for k in range(CHIPS):
        for h in range(HALVES):
            mate_copy(k, h).wait_send()
    for k in range(CHIPS - 1):
        for p in range(PIECES):
            line_copy(k, p).wait_send()


def step_at(index, step, act, cot, param, tracker, prev, moment, second):
    tokens, width = act.shape
    rows, columns = param.shape
    out = jax.ShapeDtypeStruct((rows, columns), BF16)
    anywhere = pl.BlockSpec(memory_space=pl.ANY)
    dma = pltpu.SemaphoreType.DMA
    return pl.pallas_call(
        functools.partial(kernel, index),
        out_shape=[out] * 5,
        in_specs=[anywhere] * 8,
        out_specs=[pl.BlockSpec(memory_space=pltpu.VMEM)] * 5,
        scratch_shapes=[
            pltpu.VMEM((CHIPS, 2, tokens, rows), BF16),
            pltpu.VMEM((tokens, columns), BF16),
            pltpu.VMEM((CHIPS, rows, columns), F32),
            pltpu.VMEM((CHIPS, rows, columns), BF16),
            pltpu.VMEM((CHIPS, rows, columns), BF16),
            pltpu.VMEM((CHIPS - 1, rows, columns), BF16),
            pltpu.VMEM((CHIPS + 1, rows, columns), BF16),
            pltpu.VMEM((2, rows, columns), BF16),
            pltpu.VMEM((5, rows, columns), BF16),
            pltpu.VMEM((2, 2, rows // PIECES, columns), BF16),
            pltpu.SMEM((1,), jnp.int32),
            dma((CHIPS, 2)),
            dma,
            dma((5,)),
            dma,
            dma((CHIPS, HALVES)),
            dma((CHIPS, HALVES)),
            dma((CHIPS - 1, PIECES)),
            dma((CHIPS + 1, PIECES)),
            dma((2, PIECES)),
            dma((2, PIECES)),
            dma((GROUPS - 1, 2)),
            dma((GROUPS - 2, 2)),
            pltpu.SemaphoreType.REGULAR,
        ],
        compiler_params=pltpu.CompilerParams(
            collective_id=index, has_side_effects=True, vmem_limit_bytes=40 * 2**20
        ),
        name=f"step_{index}",
    )(step, act, cot, param, tracker, prev, moment, second)


def settle_kernel(*refs):
    ins, outs, sem = refs[:5], refs[5:10], refs[10]
    copies = [
        pltpu.make_async_copy(ins[n], outs[n], sem.at[n]) for n in range(5)
    ]
    for copy in copies:
        copy.start()
    for copy in copies:
        copy.wait()


def settle(values):
    rows, columns = values[0].shape
    return pl.pallas_call(
        settle_kernel,
        out_shape=[jax.ShapeDtypeStruct((rows, columns), BF16)] * 5,
        in_specs=[pl.BlockSpec(memory_space=pltpu.VMEM)] * 5,
        out_specs=[pl.BlockSpec(memory_space=pl.ANY)] * 5,
        scratch_shapes=[pltpu.SemaphoreType.DMA((5,))],
        compiler_params=pltpu.CompilerParams(vmem_limit_bytes=4 * 2**20),
        name="settle",
    )(*values)


def body(activations, cotangent, param, tracker, prev_grad, moment, second, step):
    levels = lax.axis_size("rep").bit_length() - 1
    values = lax.switch(
        step[0] % levels,
        [functools.partial(step_at, index) for index in range(levels)],
        step,
        activations[0],
        cotangent[0],
        param[0],
        tracker[0],
        prev_grad[0],
        moment[0],
        second[0],
    )
    return tuple(value[None] for value in settle(values))


def solution(mesh):
    spread = P("rep", "fsdp", None)
    return jax.shard_map(
        body,
        mesh=mesh,
        in_specs=(spread,) * 7 + (P(),),
        out_specs=(spread,) * 5,
        check_vma=False,
    )
```

```python
import functools
import math

import jax
import jax.numpy as jnp
from jax import lax
from jax.experimental import pallas as pl
from jax.experimental.pallas import tpu as pltpu
from jax.sharding import PartitionSpec as P

beta_one = 0.9
beta_two = 0.95
learn_rate = 0.002
epsilon_value = 1e-08

MESH = pl.DeviceIdType.MESH
CHIPS = 4
PIECES = 4
HALVES = 2
ALONG_Z = 2
GROUPS = 4
F32 = jnp.float32
BF16 = jnp.bfloat16


def kernel(
    index,
    step_hbm,
    act_hbm,
    cot_hbm,
    param_hbm,
    tracker_hbm,
    prev_hbm,
    moment_hbm,
    second_hbm,
    param_out,
    tracker_out,
    moment_out,
    second_out,
    grad_out,
    act,
    cot,
    acc,
    mate_send,
    mate_recv,
    line_send,
    line_recv,
    far,
    state,
    relay,
    step_smem,
    act_sem,
    cot_sem,
    state_sem,
    step_sem,
    mate_ssem,
    mate_rsem,
    line_ssem,
    line_rsem,
    far_ssem,
    far_rsem,
    relay_ssem,
    relay_rsem,
    ready,
):
    reps = lax.axis_size("rep")
    rep = lax.axis_index("rep")
    col = lax.axis_index("fsdp")
    z = col // 2
    core = col % 2
    mate = (rep, col + 1 - 2 * core)
    shift = 1 << index
    far_to = (lax.rem(rep + shift, reps), col)
    far_from = (lax.rem(rep + reps - shift, reps), col)
    rows = param_hbm.shape[0]
    piece = rows // PIECES
    half = rows // HALVES
    last = CHIPS - 1

    upper = z // 2
    inner = (z + upper) % 2
    code = 27 + 72 * inner

    def dest(k):
        plain = (code // (4**k)) % 4 if isinstance(k, int) else lax.shift_right_logical(code, 2 * k) % 4
        return plain + upper * (last - 2 * plain)

    barrier = pltpu.get_barrier_semaphore()
    pl.semaphore_signal(barrier, inc=1, device_id=mate, device_id_type=MESH)

    @pl.when(z > 0)
    def _():
        pl.semaphore_signal(barrier, inc=1, device_id=(rep, col - 2), device_id_type=MESH)

    @pl.when(z < last)
    def _():
        pl.semaphore_signal(barrier, inc=1, device_id=(rep, col + 2), device_id_type=MESH)

    relayed = index == 0
    if relayed:
        level = rep % GROUPS
        top = GROUPS - 1
        ring = rep - level
        below = (ring + (level + GROUPS - 1) % GROUPS, col)
        above = (ring + (level + 1) % GROUPS, col)
        finally_to = ((ring + (level + GROUPS - 2) % GROUPS + shift) % reps, col)
        origin = (rep + reps - shift) % reps
        brought_by = (origin - origin % GROUPS + (origin + 2) % GROUPS, col)
        expected = 1 + jnp.where(level > 0, 3, 0) + jnp.where(level == top, 3, 0)

        @pl.when(level < top)
        def _():
            for device in (far_to, above, brought_by):
                pl.semaphore_signal(barrier, inc=1, device_id=device, device_id_type=MESH)

        @pl.when(level == 0)
        def _():
            for device in (far_from, below, finally_to):
                pl.semaphore_signal(barrier, inc=1, device_id=device, device_id_type=MESH)

    else:
        expected = 2
        pl.semaphore_signal(barrier, inc=1, device_id=far_from, device_id_type=MESH)

    def act_load(k, own):
        side = 1 - core if own == 0 else core
        start = pl.multiple_of((2 * dest(k) + side) * rows, rows)
        return pltpu.make_async_copy(
            act_hbm.at[:, pl.ds(start, rows)], act.at[k, own], act_sem.at[k, own]
        )

    cot_load = pltpu.make_async_copy(cot_hbm, cot, cot_sem)
    cot_load.start()
    act_load(0, 0).start()
    act_load(0, 1).start()
    state_loads = [
        pltpu.make_async_copy(ref, state.at[n], state_sem.at[n])
        for n, ref in enumerate((param_hbm, tracker_hbm, prev_hbm, moment_hbm, second_hbm))
    ]
    step_load = pltpu.make_async_copy(step_hbm, step_smem, step_sem)

    def later_loads():
        for k in range(1, CHIPS):
            for own in range(2):
                act_load(k, own).start()
            if k == 1:
                for load in state_loads[:2]:
                    load.start()
        for load in state_loads[2:]:
            load.start()
        step_load.start()

    def far_copy(n, p):
        part = pl.ds(p * piece, piece)
        return pltpu.make_async_remote_copy(
            src_ref=state.at[n, part],
            dst_ref=far.at[n, part],
            send_sem=far_ssem.at[n, p],
            recv_sem=far_rsem.at[n, p],
            device_id=far_to,
            device_id_type=MESH,
        )

    def mate_copy(k, h):
        part = pl.ds(h * half, half)
        return pltpu.make_async_remote_copy(
            src_ref=mate_send.at[k, part],
            dst_ref=mate_recv.at[k, part],
            send_sem=mate_ssem.at[k, h],
            recv_sem=mate_rsem.at[k, h],
            device_id=mate,
            device_id_type=MESH,
        )

    def relay_copy(hop, n):
        part = pl.ds((PIECES - 1) * piece, piece)
        ends = hop == GROUPS - 2
        return pltpu.make_async_remote_copy(
            src_ref=relay.at[hop - 1, n] if hop else state.at[n, part],
            dst_ref=far.at[n, part] if ends else relay.at[hop, n],
            send_sem=relay_ssem.at[hop, n],
            recv_sem=far_rsem.at[n, PIECES - 1] if ends else relay_rsem.at[hop, n],
            device_id=finally_to if ends else below,
            device_id_type=MESH,
        )

    def term(k, own):
        return lax.dot_general(
            act[k, own], cot[...], (((0,), (0,)), ((), ())), preferred_element_type=F32
        )

    def line_copy(k, p):
        d = dest(k)
        way = jnp.where(d > z, 1, -1)
        slot = jnp.where((d == z + way) & (way < 0), CHIPS, d)
        part = pl.ds(p * piece, piece)
        return pltpu.make_async_remote_copy(
            src_ref=line_send.at[k, part],
            dst_ref=line_recv.at[slot, part],
            send_sem=line_ssem.at[k, p],
            recv_sem=line_rsem.at[slot, p],
            device_id=(rep, col + 2 * way),
            device_id_type=MESH,
        )

    def arrival(slot, p):
        part = pl.ds(p * piece, piece)
        return pltpu.make_async_remote_copy(
            src_ref=line_send.at[0, part],
            dst_ref=line_recv.at[slot, part],
            send_sem=line_ssem.at[0, p],
            recv_sem=line_rsem.at[slot, p],
            device_id=mate,
            device_id_type=MESH,
        )

    def wait_barrier():
        ends = jnp.where(z > 0, 1, 0) + jnp.where(z < last, 1, 0)
        pl.semaphore_wait(barrier, expected + ends)
        if relayed:

            @pl.when(level > 0)
            def _():
                pl.semaphore_signal(ready, inc=1, device_id=far_from, device_id_type=MESH)

            @pl.when(level == top)
            def _():
                for device in (above, brought_by):
                    pl.semaphore_signal(ready, inc=1, device_id=device, device_id_type=MESH)

    def compute(k):
        act_load(k, 0).wait()

        @pl.when(k == 0)
        def _():
            later_loads()

        mate_send[k] = term(k, 0).astype(BF16)

        @pl.when(k == 0)
        def _():
            wait_barrier()

        for h in range(HALVES):
            mate_copy(k, h).start()

        act_load(k, 1).wait()
        acc[k] = term(k, 1)

        @pl.when(k == 0)
        def _():
            for load in state_loads[:2]:
                load.wait()
            if relayed:

                @pl.when(level > 0)
                def _():
                    for n in range(2):
                        relay_copy(0, n).start()

            if index >= ALONG_Z:
                for n in range(2):
                    for p in range(PIECES):
                        far_copy(n, p).start()

    def pass_on(k):
        d = dest(k)
        way = jnp.where(d > z, 1, -1)
        behind = z - way
        fed = (behind >= 0) & (behind <= last)
        for p in range(PIECES):
            part = pl.ds(p * piece, piece)
            if p % (PIECES // HALVES) == 0:
                mate_copy(k, p // (PIECES // HALVES)).wait_recv()
            own = acc[k, part] + mate_recv[k, part].astype(F32)

            @pl.when(fed)
            def _():
                arrival(d, p).wait_recv()
                line_send[k, part] = (own + line_recv[d, part].astype(F32)).astype(BF16)

            @pl.when(jnp.logical_not(fed))
            def _():
                line_send[k, part] = own.astype(BF16)

            line_copy(k, p).start()
            if index < ALONG_Z and not relayed:
                turn = k * PIECES + p

                @pl.when(turn < 2 * PIECES)
                def _():
                    far_copy(turn % 2, turn // 2).start()

        if relayed:

            @pl.when((k == 0) & (level > 0) & (level < top))
            def _():
                pl.semaphore_wait(ready, 1)

            @pl.when((level > 0) & (k == 0))
            def _():
                for p in range(PIECES - 1):
                    for n in range(2):
                        far_copy(n, p).start()

            @pl.when((k == 1) & (level > 0))
            def _():
                for n in range(2):
                    relay_copy(0, n).wait_recv()
                    relay_copy(1, n).start()

            @pl.when((k == 1) & (level == 0))
            def _():
                pl.semaphore_wait(ready, 3)
                for n in range(2):
                    relay_copy(0, n).start()
                for p in range(PIECES - 1):
                    for n in range(2):
                        far_copy(n, p).start()

            @pl.when((k == 2) & (level == 0))
            def _():
                for n in range(2):
                    relay_copy(0, n).wait_recv()
                    relay_copy(1, n).start()

            @pl.when(k == 2)
            def _():
                for n in range(2):
                    relay_copy(1, n).wait_recv()
                    relay_copy(2, n).start()

    cot_load.wait()

    def step(i, carry):
        @pl.when(i < CHIPS)
        def _():
            compute(i)

        @pl.when(i < CHIPS - 1)
        def _():
            pass_on(i)

        return carry

    lax.fori_loop(0, CHIPS, step, 0)

    for load in state_loads[2:]:
        load.wait()
    step_load.wait()
    count = jnp.full((1, param_hbm.shape[1]), step_smem[0] + 1, jnp.int32).astype(F32)
    scale_one = 1.0 / (1.0 - jnp.exp(count * math.log(beta_one)))
    scale_two = 1.0 / (1.0 - jnp.exp(count * math.log(beta_two)))

    def finish(p, carry):
        part = pl.ds(pl.multiple_of(p * piece, piece), piece)

        for n in range(2):
            far_copy(n, p).wait_recv()

        @pl.when(p % (PIECES // HALVES) == 0)
        def _():
            mate_copy(last, p // (PIECES // HALVES)).wait_recv()

        acc[last, part] += mate_recv[last, part].astype(F32)

        @pl.when(z > 0)
        def _():
            arrival(z, p).wait_recv()
            acc[last, part] += line_recv[z, part].astype(F32)

        @pl.when(z < last)
        def _():
            arrival(CHIPS, p).wait_recv()
            acc[last, part] += line_recv[CHIPS, part].astype(F32)

        grad = acc[last, part]
        mixed_param = 0.5 * (state[0, part].astype(F32) + far[0, part].astype(F32))
        mixed_tracker = 0.5 * (state[1, part].astype(F32) + far[1, part].astype(F32))
        new_tracker = mixed_tracker + grad - state[2, part].astype(F32)
        new_moment = beta_one * state[3, part].astype(F32) + (1.0 - beta_one) * new_tracker
        new_second = (
            beta_two * state[4, part].astype(F32) + (1.0 - beta_two) * new_tracker * new_tracker
        )
        update = (new_moment * scale_one) / (jnp.sqrt(new_second * scale_two) + epsilon_value)
        param_out[part] = (mixed_param - learn_rate * update).astype(BF16)
        tracker_out[part] = new_tracker.astype(BF16)
        moment_out[part] = new_moment.astype(BF16)
        second_out[part] = new_second.astype(BF16)
        grad_out[part] = grad.astype(BF16)
        return carry

    lax.fori_loop(0, PIECES, finish, 0)

    for n in range(2):
        for p in range(PIECES):
            if relayed and p == PIECES - 1:
                for hop in range(GROUPS - 1):
                    relay_copy(hop, n).wait_send()
            else:
                far_copy(n, p).wait_send()
    for k in range(CHIPS):
        for h in range(HALVES):
            mate_copy(k, h).wait_send()
    for k in range(CHIPS - 1):
        for p in range(PIECES):
            line_copy(k, p).wait_send()


def step_at(index, step, act, cot, param, tracker, prev, moment, second):
    tokens, width = act.shape
    rows, columns = param.shape
    out = jax.ShapeDtypeStruct((rows, columns), BF16)
    anywhere = pl.BlockSpec(memory_space=pl.ANY)
    dma = pltpu.SemaphoreType.DMA
    return pl.pallas_call(
        functools.partial(kernel, index),
        out_shape=[out] * 5,
        in_specs=[anywhere] * 8,
        out_specs=[pl.BlockSpec(memory_space=pltpu.VMEM)] * 5,
        scratch_shapes=[
            pltpu.VMEM((CHIPS, 2, tokens, rows), BF16),
            pltpu.VMEM((tokens, columns), BF16),
            pltpu.VMEM((CHIPS, rows, columns), F32),
            pltpu.VMEM((CHIPS, rows, columns), BF16),
            pltpu.VMEM((CHIPS, rows, columns), BF16),
            pltpu.VMEM((CHIPS - 1, rows, columns), BF16),
            pltpu.VMEM((CHIPS + 1, rows, columns), BF16),
            pltpu.VMEM((2, rows, columns), BF16),
            pltpu.VMEM((5, rows, columns), BF16),
            pltpu.VMEM((2, 2, rows // PIECES, columns), BF16),
            pltpu.SMEM((1,), jnp.int32),
            dma((CHIPS, 2)),
            dma,
            dma((5,)),
            dma,
            dma((CHIPS, HALVES)),
            dma((CHIPS, HALVES)),
            dma((CHIPS - 1, PIECES)),
            dma((CHIPS + 1, PIECES)),
            dma((2, PIECES)),
            dma((2, PIECES)),
            dma((GROUPS - 1, 2)),
            dma((GROUPS - 2, 2)),
            pltpu.SemaphoreType.REGULAR,
        ],
        compiler_params=pltpu.CompilerParams(
            collective_id=index, has_side_effects=True, vmem_limit_bytes=40 * 2**20
        ),
        name=f"step_{index}",
    )(step, act, cot, param, tracker, prev, moment, second)


def settle_kernel(*refs):
    ins, outs, sem = refs[:5], refs[5:10], refs[10]
    copies = [
        pltpu.make_async_copy(ins[n], outs[n], sem.at[n]) for n in range(5)
    ]
    for copy in copies:
        copy.start()
    for copy in copies:
        copy.wait()


def settle(values):
    rows, columns = values[0].shape
    return pl.pallas_call(
        settle_kernel,
        out_shape=[jax.ShapeDtypeStruct((rows, columns), BF16)] * 5,
        in_specs=[pl.BlockSpec(memory_space=pltpu.VMEM)] * 5,
        out_specs=[pl.BlockSpec(memory_space=pl.ANY)] * 5,
        scratch_shapes=[pltpu.SemaphoreType.DMA((5,))],
        compiler_params=pltpu.CompilerParams(vmem_limit_bytes=4 * 2**20),
        name="settle",
    )(*values)


def body(activations, cotangent, param, tracker, prev_grad, moment, second, step):
    levels = lax.axis_size("rep").bit_length() - 1
    values = lax.switch(
        step[0] % levels,
        [functools.partial(step_at, index) for index in range(levels)],
        step,
        activations[0],
        cotangent[0],
        param[0],
        tracker[0],
        prev_grad[0],
        moment[0],
        second[0],
    )
    return tuple(value[None] for value in settle(values))


def solution(mesh):
    spread = P("rep", "fsdp", None)
    return jax.shard_map(
        body,
        mesh=mesh,
        in_specs=(spread,) * 7 + (P(),),
        out_specs=(spread,) * 5,
        check_vma=False,
    )
```
